32 devices in a mesh: node: 2 (over y), sub: 16 (over z, x, core).
Axes of the slice: x: 2, y: 2, z: 4, core: 2. Of those that a mesh axis runs over, the one named last changes fastest.
Arguments:
- inner_inverse: bfloat16 [2, 16, 2, 1024, 1024], P('node', 'sub'), may hold values from -1 to 2
- schur_inverse: bfloat16 [2, 2, 2048, 2048], P('node', None, 'sub'), may hold values from -1 to 2
- coupling: bfloat16 [16, 1024, 128], P('sub'), may hold values from -0.5 to 0.5
- iface_index: int32 [16, 128], P('sub'), may hold values from 0 to 2047, as said below
- basis_inner: bfloat16 [16384, 384], P('sub'), may hold values from -2134 to 2134
- basis_iface: bfloat16 [2048, 384], P('sub'), may hold values from -134 to 134
- node_weights: float32 [2, 2], P('node'), may hold values from -4 to 4
Outputs:
- filtered_inner: float32 [16384, 384], P('sub')
- filtered_iface: float32 [2048, 384], P('sub')
The draws below stay inside these ranges and needn't reach their ends.
Inputs may be any that keep to these rules, and one draw needn't show every extreme that they name: `iface_index`: over all rows every interface unknown from 0 to 2047 appears exactly once.
All inputs are finite; a program needn't handle non-finite values.
Results may differ from the reference program's by a relative error of at most 0.0086.
Values may be sent and summed in bfloat16 or wider, within the bound.
A program may use at most 64 MiB of HBM per device.

```python
import math
import jax
import jax.numpy as jnp
from jax import lax

NI = 1024
LG = 128
M = 384
NODES = 2
SUBS = 16
NGT = 2048
INNER = 16384
ROWS = 18432


def scaled_basis(key, row_count, rising):
    key_base, key_rows, key_cols = jax.random.split(key, 3)
    row_scale = jnp.exp(jax.random.uniform(key_rows, (row_count, 1), jnp.float32, 0.0, math.log(10.0)))
    col_scale = jnp.exp(jax.random.uniform(key_cols, (1, M), jnp.float32, 0.0, math.log(10.0)))
    base = jax.random.normal(key_base, (row_count, M), jnp.float32)
    base = jnp.clip(base, -4.0, 4.0)
    if rising:
        block_number = (jnp.arange(row_count, dtype=jnp.int32) // NI).astype(jnp.float32)
        trend = jnp.exp(math.log(16.0) * block_number / max(SUBS - 1, 1))
        row_scale = row_scale * trend[:, None]
    return (base * row_scale * col_scale / 3.0).astype(jnp.bfloat16)


def dominant_blocks(key, lead_shape, order):
    key_noise, key_real, key_imag = jax.random.split(key, 3)
    full_shape = lead_shape + (2, order, order)
    spread = 0.5 / math.sqrt(order)
    noise = jnp.clip(jax.random.normal(key_noise, full_shape, jnp.float32), -4.0, 4.0)
    diag_real = jax.random.uniform(key_real, lead_shape + (1, order), jnp.float32, 0.8, 1.6)
    diag_imag = jax.random.uniform(key_imag, lead_shape + (1, order), jnp.float32, -0.6, 0.6)
    diag_both = jnp.concatenate([diag_real, diag_imag], axis=-2)
    rows = jax.lax.broadcasted_iota(jnp.int32, (order, order), 0)
    cols = jax.lax.broadcasted_iota(jnp.int32, (order, order), 1)
    identity = (rows == cols).astype(jnp.float32)
    return (spread * noise + diag_both[..., :, None] * identity).astype(jnp.bfloat16)


def draw_inner_inverse(key, part):
    return dominant_blocks(jax.random.fold_in(key, 31), (NODES, SUBS), NI)


def draw_schur_inverse(key, part):
    blocks = dominant_blocks(jax.random.fold_in(key, 37), (NODES,), NGT)
    return blocks


def draw_basis_inner(key, part):
    return scaled_basis(jax.random.fold_in(key, 11), INNER, True)


def draw_basis_iface(key, part):
    return scaled_basis(jax.random.fold_in(key, 23), NGT, False)


def draw_iface_index(key, part):
    order = jax.random.permutation(jax.random.fold_in(key, 5), NGT)
    return order.reshape(SUBS, LG).astype(jnp.int32)


def block_scale(rng, dims, cuts, smallest, largest):
    factor_of, own = 1.0, jax.random.fold_in(rng, 6)
    for axis_at, shards_of in cuts:
        steps = jnp.exp(jax.random.uniform(jax.random.fold_in(own, axis_at), (shards_of,), jnp.float32, smallest / len(cuts), largest / len(cuts)))
        factor_of = factor_of * jnp.repeat(steps, dims[axis_at] // shards_of).reshape([-1 if axis == axis_at else 1 for axis in range(len(dims))])
    return factor_of


def normal_values(own_key, shape, deviation, most, shards=(), held_as=jnp.bfloat16):
    factor_of = block_scale(own_key, shape, shards, -0.22, 0.18) if shards else 1.0
    values = jax.random.normal(own_key, shape, jnp.float32) * deviation * factor_of
    return jnp.minimum(jnp.maximum(values, -most), most).astype(held_as)


def setup_inputs(seed: int = 0) -> dict:
    streams_of = jax.random.split(jax.random.key(seed), 8)
    return {
        "inner_inverse": draw_inner_inverse(jax.random.fold_in(streams_of[7], 71), 0),
        "schur_inverse": draw_schur_inverse(jax.random.fold_in(streams_of[7], 71), 0),
        "coupling": normal_values(streams_of[2], (SUBS, NI, LG), LG ** -0.5, 0.5, ((0, 16),)),
        "iface_index": draw_iface_index(jax.random.fold_in(streams_of[7], 71), 0),
        "basis_inner": draw_basis_inner(jax.random.fold_in(streams_of[7], 71), 0),
        "basis_iface": draw_basis_iface(jax.random.fold_in(streams_of[7], 71), 0),
        "node_weights": normal_values(streams_of[6], (NODES, 2), 1.0, 4.0, ((0, 2),), jnp.float32),
    }


def reference(inner_inverse, schur_inverse, coupling, iface_index, basis_inner, basis_iface, node_weights):
    basis_blocks = basis_inner.reshape(SUBS, NI, M)
    flat_index = iface_index.reshape(-1).astype(jnp.int32)
    filt_inner = jnp.zeros((SUBS, NI, M), jnp.float32)
    filt_iface = jnp.zeros((NGT, M), jnp.float32)
    for node_number in range(NODES):
        weight_real = node_weights[node_number, 0]
        weight_imag = node_weights[node_number, 1]

        def first_section(operands):
            inverse_block, base_block, couple_block = operands
            solve_block = jnp.dot(inverse_block.reshape(2 * NI, NI).astype(jnp.float32), base_block.astype(jnp.float32), preferred_element_type=jnp.float32).astype(jnp.bfloat16)
            contrib = jnp.einsum('il,cim->lcm', couple_block.astype(jnp.float32), solve_block.reshape(2, NI, M).astype(jnp.float32))
            return (solve_block, contrib.astype(jnp.bfloat16).reshape(LG, 2 * M))
        solves, contribs = lax.map(first_section, (inner_inverse[node_number], basis_blocks, coupling))
        summed = jnp.zeros((NGT, 2 * M), jnp.float32).at[flat_index].add(contribs.reshape(SUBS * LG, 2 * M).astype(jnp.float32))
        right_side = jnp.concatenate([basis_iface.astype(jnp.float32) - summed[:, :M], -summed[:, M:]], axis=1).astype(jnp.bfloat16)
        from_real = jnp.dot(schur_inverse[node_number, 0].astype(jnp.float32), right_side.astype(jnp.float32), preferred_element_type=jnp.float32)
        from_imag = jnp.dot(schur_inverse[node_number, 1].astype(jnp.float32), right_side.astype(jnp.float32), preferred_element_type=jnp.float32)
        solution = jnp.concatenate([from_real[:, :M] - from_imag[:, M:], from_real[:, M:] + from_imag[:, :M]], axis=1).astype(jnp.bfloat16)
        picked = solution[iface_index.astype(jnp.int32)]

        def second_section(operands):
            inverse_block, couple_block, solve_block, picked_block = operands
            correction = jnp.dot(couple_block.astype(jnp.float32), picked_block.astype(jnp.float32), preferred_element_type=jnp.float32).astype(jnp.bfloat16)
            inner_fix = jnp.dot(inverse_block.reshape(2 * NI, NI).astype(jnp.float32), correction.astype(jnp.float32), preferred_element_type=jnp.float32)
            fix_real = inner_fix[:NI, :M] - inner_fix[NI:, M:]
            fix_imag = inner_fix[:NI, M:] + inner_fix[NI:, :M]
            full_real = solve_block[:NI].astype(jnp.float32) - fix_real
            full_imag = solve_block[NI:].astype(jnp.float32) - fix_imag
            return weight_real * full_real - weight_imag * full_imag
        filt_inner = filt_inner + lax.map(second_section, (inner_inverse[node_number], coupling, solves, picked))
        solution_wide = solution.astype(jnp.float32)
        filt_iface = filt_iface + (weight_real * solution_wide[:, :M] - weight_imag * solution_wide[:, M:])
    filt_flat = filt_inner.reshape(INNER, M)
    gram_matrix = jnp.einsum('rm,rn->mn', filt_flat, filt_flat, precision=lax.Precision.HIGHEST)
    gram_matrix = gram_matrix + jnp.einsum('rm,rn->mn', filt_iface, filt_iface, precision=lax.Precision.HIGHEST)
    gram_matrix = gram_matrix / ROWS
    lower_factor = jnp.linalg.cholesky(gram_matrix)
    filtered_inner = lax.linalg.triangular_solve(lower_factor, filt_flat, left_side=False, lower=True, transpose_a=True)
    filtered_iface = lax.linalg.triangular_solve(lower_factor, filt_iface, left_side=False, lower=True, transpose_a=True)
    return (filtered_inner, filtered_iface)
```

```python
import functools
import jax
import jax.numpy as jnp
from jax import lax
from jax.experimental import pallas as pl
from jax.experimental.pallas import tpu as pltpu
from jax.sharding import PartitionSpec as P

MESH = pl.DeviceIdType.MESH
LANE = 128
F32 = jnp.float32
BF16 = jnp.bfloat16
TN = (((0,), (0,)), ((), ()))
NT = (((1,), (1,)), ((), ()))


class Gather:
    def __init__(self, na, nb, buf, send, recv):
        self.na, self.nb, self.buf, self.send, self.recv = na, nb, buf, send, recv
        node = lax.axis_index("node")
        me = lax.axis_index("sub")
        self.a = me // (2 * nb)
        self.b = (me // 2) % nb
        self.c = me % 2
        self.node = node
        self.me = me

    def slot(self, a, b, c):
        return (a * self.nb + b) * 2 + c

    def copy(self, origin, kind, place, target):
        return pltpu.make_async_remote_copy(
            src_ref=self.buf.at[origin],
            dst_ref=self.buf.at[origin],
            send_sem=self.send.at[kind, place],
            recv_sem=self.recv.at[origin],
            device_id=(self.node, target),
            device_id_type=MESH,
        )

    def routes(self, oa, ob):
        a, b = self.a, self.b
        return (
            (0, (ob == b) & (oa <= a) & (a + 1 < self.na), self.slot(a + 1, b, self.c)),
            (1, (ob == b) & (oa >= a) & (a >= 1), self.slot(a - 1, b, self.c)),
            (2, (ob <= b) & (b + 1 < self.nb), self.slot(a, b + 1, self.c)),
            (3, (ob >= b) & (b >= 1), self.slot(a, b - 1, self.c)),
        )

    def handle(self, oa, ob, own):
        origin = self.slot(oa, ob, self.c)
        place = oa * self.nb + ob
        sibling = self.slot(self.a, self.b, 1 - self.c)
        if not own:
            self.copy(origin, 4, place, sibling).wait_recv()
        for kind, cond, target in self.routes(oa, ob):

            @pl.when(cond)
            def _(kind=kind, target=target):
                self.copy(origin, kind, place, target).start()

        self.copy(origin, 4, place, sibling).start()

    def step(self, tau):
        if tau == 0:
            self.handle(self.a, self.b, True)
            return
        for tb in range(self.nb):
            t = tau - tb
            if t < 0 or t >= self.na:
                continue
            for sa in (-1, 1) if t else (1,):
                for sb in (-1, 1) if tb else (1,):
                    oa, ob = self.a + sa * t, self.b + sb * tb
                    ok = (oa >= 0) & (oa < self.na) & (ob >= 0) & (ob < self.nb)

                    @pl.when(ok)
                    def _(oa=oa, ob=ob):
                        self.handle(oa, ob, False)

    @property
    def steps(self):
        return self.na + self.nb - 1

    def finish(self):
        sibling = self.slot(self.a, self.b, 1 - self.c)

        @pl.loop(0, self.na * self.nb)
        def _(place):
            oa, ob = place // self.nb, place % self.nb
            self.copy(place * 2 + 1 - self.c, 4, place, sibling).wait_recv()
            for kind, cond, target in self.routes(oa, ob):

                @pl.when(cond)
                def _(kind=kind, target=target):
                    self.copy(place * 2 + self.c, kind, place, target).wait_send()

            self.copy(place * 2 + self.c, 4, place, sibling).wait_send()


def step_kernel(
    dims, inv_hbm, schur_hbm, couple, index, basis_in, basis_if, weights,
    filt, gbuf,
    inv, schur, solve, idx_all, bas_all, con_all, sol_all, sperm, work, term, tsend, trecv, g6, grecv, nrecv,
    ld, isend, irecv, bsend, brecv, csend, crecv, ssend, srecv, tss, trs, fss, frs, gss, grs, nss, nrs, ass_, ars,
):
    na, nb, nodes = dims
    subs = na * nb * 2
    ni = inv.shape[1]
    m = basis_in.shape[1]
    lg = couple.shape[1]
    total = schur.shape[2]
    rows = ni + lg
    ch = rows // nodes
    node = lax.axis_index("node")
    me = lax.axis_index("sub")

    load_inv = pltpu.make_async_copy(inv_hbm, inv, ld.at[0])
    load_schur = pltpu.make_async_copy(schur_hbm, schur, ld.at[1])
    put_idx = pltpu.make_async_copy(index, idx_all.at[me], ld.at[2])
    put_bas = pltpu.make_async_copy(basis_if, bas_all.at[me], ld.at[3])
    load_inv.start()
    put_idx.start()
    put_bas.start()
    load_schur.start()

    gi = Gather(na, nb, idx_all, isend, irecv)
    gb = Gather(na, nb, bas_all, bsend, brecv)
    gc = Gather(na, nb, con_all, csend, crecv)
    gs = Gather(na, nb, sol_all, ssend, srecv)
    gg = Gather(na, nb, gbuf, ass_, ars)

    barrier = pltpu.get_barrier_semaphore()
    a, b, c = gi.a, gi.b, gi.c
    links = (
        (a + 1 < na, gi.slot(a + 1, b, c)),
        (a >= 1, gi.slot(a - 1, b, c)),
        (b + 1 < nb, gi.slot(a, b + 1, c)),
        (b >= 1, gi.slot(a, b - 1, c)),
    )
    for cond, target in links:

        @pl.when(cond)
        def _(target=target):
            pl.semaphore_signal(barrier, inc=1, device_id=(node, target), device_id_type=MESH)

    pl.semaphore_signal(barrier, inc=1, device_id=(node, gi.slot(a, b, 1 - c)), device_id_type=MESH)
    for p in range(1, nodes):
        pl.semaphore_signal(
            barrier, inc=1, device_id=((node + p) % nodes, me), device_id_type=MESH
        )
    count = nodes
    for cond, _t in links:
        count = count + cond.astype(jnp.int32)
    pl.semaphore_wait(barrier, count)
    put_idx.wait()
    gi.step(0)
    put_bas.wait()
    gb.step(0)
    load_inv.wait()

    cr = 256
    per_part = ni // cr
    chunks = 2 * per_part
    y = basis_in[...]

    def solve_chunk(q, _):
        part = q // per_part
        r0 = pl.multiple_of((q % per_part) * cr, cr)
        out = jnp.dot(inv[part, pl.ds(r0, cr), :], y, preferred_element_type=F32)
        solve[part, pl.ds(r0, cr), :] = out.astype(BF16)
        return 0

    lax.fori_loop(0, chunks, solve_chunk, 0)
    for part in range(2):
        out = lax.dot_general(couple[...], solve[part], TN, preferred_element_type=F32)
        con_all[me, :, pl.ds(part * m, m)] = out.astype(BF16)
    gc.step(0)
    for tau in range(1, gi.steps):
        gi.step(tau)
    gi.finish()
    for tau in range(1, gb.steps):
        gb.step(tau)
        if tau < 2:
            gc.step(tau)

    load_schur.wait()
    s2 = schur[...].reshape(2 * lg, total)

    def perm_pair(q, _):
        iota = lax.broadcasted_iota(jnp.int32, (total, LANE), 0)
        hot = jnp.concatenate(
            [(iota == idx_all[2 * q + k]).astype(BF16) for k in range(2)], axis=1
        )
        got = jnp.dot(s2, hot, preferred_element_type=F32)
        sperm[q] = got.astype(BF16)
        return 0

    lax.fori_loop(0, subs // 2, perm_pair, 0)
    for tau in range(2, gc.steps):
        gc.step(tau)
    gb.finish()
    base = jnp.dot(s2, bas_all[...].reshape(total, m), preferred_element_type=F32)
    gc.finish()

    work[...] = jnp.zeros_like(work)

    @pl.loop(0, subs // 2)
    def _(q):
        rhs = con_all[pl.ds(2 * q, 2)].reshape(2 * lg, 2 * m)
        work[...] += jnp.dot(sperm[q], rhs, preferred_element_type=F32)

    sol_re = base[:lg] - work[:lg, :m] + work[lg:, m:]
    sol_im = base[lg:] - work[:lg, m:] - work[lg:, :m]
    sol_all[me, :, pl.ds(0, m)] = sol_re.astype(BF16)
    sol_all[me, :, pl.ds(m, m)] = sol_im.astype(BF16)
    gs.step(0)
    wr = weights[node * 0, 0]
    wi = weights[node * 0, 1]
    t_if = wr * sol_re.astype(BF16).astype(F32) - wi * sol_im.astype(BF16).astype(F32)
    term[pl.ds(ni, lg), :] = t_if
    tsend[pl.ds(ni, lg), :] = t_if.astype(BF16)
    rowid = jnp.broadcast_to(index[...], (LANE, LANE)).T
    for tau in range(1, gs.steps):
        gs.step(tau)
    gs.finish()

    lanes = lax.broadcasted_iota(jnp.int32, (LANE, LANE), 1)
    sel = jnp.concatenate(
        [(lanes + LANE * k == rowid).astype(BF16) for k in range(total // LANE)], axis=1
    )
    picked = jnp.dot(sel, sol_all[...].reshape(total, 2 * m), preferred_element_type=F32).astype(BF16)

    def pq_chunk(q, _):
        r0 = pl.multiple_of(q * cr, cr)
        cor = jnp.dot(couple[pl.ds(r0, cr), :], picked, preferred_element_type=F32)
        d_re = basis_in[pl.ds(r0, cr), :].astype(F32) - cor[:, :m]
        d_im = cor[:, m:]
        solve[0, pl.ds(r0, cr), :] = (wr * d_re + wi * d_im).astype(BF16)
        solve[1, pl.ds(r0, cr), :] = (wr * d_im - wi * d_re).astype(BF16)
        return 0

    lax.fori_loop(0, per_part, pq_chunk, 0)

    def term_chunk(q, _):
        r0 = pl.multiple_of(q * cr, cr)
        out = jnp.dot(inv[0, pl.ds(r0, cr), :], solve[0], preferred_element_type=F32)
        out += jnp.dot(inv[1, pl.ds(r0, cr), :], solve[1], preferred_element_type=F32)
        term[pl.ds(r0, cr), :] = out
        tsend[pl.ds(r0, cr), :] = out.astype(BF16)
        return 0

    lax.fori_loop(0, per_part, term_chunk, 0)

    def share(k):
        return pl.ds(pl.multiple_of(k * ch, 16), ch)

    def term_copy(p):
        peer = (node + p) % nodes
        return pltpu.make_async_remote_copy(
            src_ref=tsend.at[share(peer)], dst_ref=trecv.at[p - 1],
            send_sem=tss.at[p - 1], recv_sem=trs.at[p - 1],
            device_id=(peer, me), device_id_type=MESH,
        )

    def filt_copy(p):
        peer = (node + p) % nodes
        return pltpu.make_async_remote_copy(
            src_ref=filt.at[share(node)], dst_ref=filt.at[share(node)],
            send_sem=fss.at[p - 1], recv_sem=frs.at[p - 1],
            device_id=(peer, me), device_id_type=MESH,
        )

    for p in range(1, nodes):
        term_copy(p).start()
    for p in range(1, nodes):
        term_copy(p).wait()
    own = term[share(node), :]
    for p in range(1, nodes):
        own += trecv[p - 1].astype(F32)
    own = own.astype(BF16)
    filt[share(node), :] = own
    for p in range(1, nodes):
        filt_copy(p).start()

    nbk = m // LANE
    at = 0
    for rb in range(nbk):
        blk = lax.dot_general(
            own[:, rb * LANE : (rb + 1) * LANE], own[:, rb * LANE :], TN, preferred_element_type=F32
        )
        for k in range(nbk - rb):
            g6[pl.ds(at * LANE, LANE), :] = blk[:, k * LANE : (k + 1) * LANE]
            at += 1
    r6 = g6.shape[0] // subs

    def piece(k):
        return pl.ds(pl.multiple_of(k * r6, 8), r6)

    def gram_copy(p):
        peer = (me + p) % subs
        return pltpu.make_async_remote_copy(
            src_ref=g6.at[piece(peer)], dst_ref=grecv.at[me],
            send_sem=gss.at[p], recv_sem=grs.at[p],
            device_id=(node, peer), device_id_type=MESH,
        )

    @pl.loop(1, subs)
    def _(p):
        gram_copy(p).start()

    grecv[me] = g6[piece(me), :]

    @pl.loop(1, subs)
    def _(p):
        gram_copy(p).wait()

    part = grecv[0]
    for k in range(1, subs):
        part += grecv[k]
    nrecv[node] = part

    def node_copy(p):
        peer = (node + p) % nodes
        return pltpu.make_async_remote_copy(
            src_ref=nrecv.at[node], dst_ref=nrecv.at[node],
            send_sem=nss.at[p - 1], recv_sem=nrs.at[p - 1],
            device_id=(peer, me), device_id_type=MESH,
        )

    for p in range(1, nodes):
        node_copy(p).start()
    for p in range(1, nodes):
        node_copy(p).wait()
    full = nrecv[0]
    for k in range(1, nodes):
        full += nrecv[k]
    gbuf[me] = full
    for tau in range(gg.steps):
        gg.step(tau)
    gg.finish()
    for p in range(1, nodes):
        filt_copy(p).wait()


def factor_kernel(scale, g6, filt, out_inner, out_iface, tw, uall, wall):
    m = filt.shape[1]
    nbk = m // LANE
    width = LANE * (nbk + 1)
    row8 = lax.broadcasted_iota(jnp.int32, (8, LANE), 0)
    groups = LANE // 8
    hi = lax.Precision.HIGHEST
    at = 0
    for blk in range(nbk):
        nu = nbk - blk
        for k in range(nu):
            tw[:, k * LANE : (k + 1) * LANE] = g6[(at + k) * LANE : (at + k + 1) * LANE, :] * scale
        at += nu
        ri = lax.broadcasted_iota(jnp.int32, (LANE, LANE), 0)
        ci = lax.broadcasted_iota(jnp.int32, (LANE, LANE), 1)
        for k in range(blk + 1):
            tile = (ri == ci).astype(F32) if k == blk else jnp.zeros((LANE, LANE), F32)
            tw[:, (nu + k) * LANE : (nu + k + 1) * LANE] = tile
        for p in range(blk):
            left = uall[p, :, blk * LANE : (blk + 1) * LANE]
            tw[:, : nu * LANE] -= lax.dot_general(
                left, uall[p, :, blk * LANE :], TN, precision=hi, preferred_element_type=F32
            )
            tw[:, nu * LANE : (nu + p + 1) * LANE] -= lax.dot_general(
                left, wall[p, :, : (p + 1) * LANE], TN, precision=hi, preferred_element_type=F32
            )

        @pl.loop(0, groups)
        def _(p):
            r0 = pl.multiple_of(8 * p, 8)
            x = tw[pl.ds(r0, 8), :]
            d = x[:, :LANE]
            cols = [jnp.broadcast_to(d[:, j : j + 1], (8, LANE)) for j in range(8)]
            tiles = [x[:, k * LANE : (k + 1) * LANE] for k in range(nbk + 1)]
            inv, low, us = [], [], []
            diag = jnp.ones((8, LANE), F32)
            for j in range(8):
                piv = jnp.broadcast_to(cols[j][j : j + 1, :], (8, LANE))
                r = lax.rsqrt(piv)
                r = r * (1.5 - 0.5 * piv * r * r)
                inv.append(r)
                lj = cols[j] * r
                lows = {}
                for k in range(j + 1, 8):
                    lows[k] = jnp.broadcast_to(lj[k : k + 1, :], (8, LANE))
                    cols[k] = cols[k] - lj * lows[k]
                low.append(lows)
                diag = jnp.where(row8 == j, r, diag)
                lm = jnp.where(row8 > j, lj, 0.0)
                u = [jnp.broadcast_to(t[j : j + 1, :], (8, LANE)) * r for t in tiles]
                us.append(u)
                tiles = [t - lm * uu for t, uu in zip(tiles, u)]
            tiles = [t * diag for t in tiles]
            for g in range(groups):
                live = (g > p).astype(F32)
                xg = tw[8 * g : 8 * g + 8, :]
                tg = [xg[:, k * LANE : (k + 1) * LANE] for k in range(nbk + 1)]
                cg = [jnp.broadcast_to(tg[0][:, j : j + 1], (8, LANE)) for j in range(8)]
                for j in range(8):
                    lj = cg[j] * (inv[j] * live)
                    for k in range(j + 1, 8):
                        cg[k] = cg[k] - lj * low[j][k]
                    tg = [t - lj * uu for t, uu in zip(tg, us[j])]
                tg[0] = pltpu.roll(tg[0], LANE - 8, 1)
                for k in range(nbk + 1):
                    tw[8 * g : 8 * g + 8, k * LANE : (k + 1) * LANE] = tg[k]
            for k in range(1, nbk + 1):
                tw[pl.ds(r0, 8), k * LANE : (k + 1) * LANE] = tiles[k]

        if nu > 1:
            uall[blk, :, (blk + 1) * LANE :] = tw[:, LANE : nu * LANE]
        wall[blk, :, : (blk + 1) * LANE] = tw[:, nu * LANE :]
        if nu > 1:
            wall[blk, :, (blk + 1) * LANE :] = jnp.zeros((LANE, (nu - 1) * LANE), F32)

    w = wall[...].reshape(m, m)
    w_hi = w.astype(BF16)
    w_lo = (w - w_hi.astype(F32)).astype(BF16)

    def apply(rows):
        out = lax.dot_general(rows, w_hi, NT, preferred_element_type=F32)
        return out + lax.dot_general(rows, w_lo, NT, preferred_element_type=F32)

    ni = out_inner.shape[0]

    @pl.loop(0, ni // LANE)
    def _(q):
        r0 = pl.multiple_of(q * LANE, LANE)
        out_inner[pl.ds(r0, LANE), :] = apply(filt[pl.ds(r0, LANE), :])

    out_iface[...] = apply(filt[pl.ds(ni, LANE), :])


def per_device(
    inner_inverse, schur_inverse, coupling, iface_index, basis_inner, basis_iface, node_weights
):
    subs, nodes = lax.axis_size("sub"), lax.axis_size("node")
    na = 4
    nb = subs // (2 * na)
    ni, m = basis_inner.shape
    lg = basis_iface.shape[0]
    total = schur_inverse.shape[3]
    rows = ni + lg
    ch = rows // nodes
    nbk = m // LANE
    n6 = nbk * (nbk + 1) // 2 * LANE
    r6 = n6 // subs
    vm = pl.BlockSpec(memory_space=pltpu.VMEM)
    hbm = pl.BlockSpec(memory_space=pl.ANY)
    dma = pltpu.SemaphoreType.DMA

    def pair():
        return [dma((5, subs // 2)), dma((subs,))]

    peers = max(nodes - 1, 1)
    filt, gram = pl.pallas_call(
        functools.partial(step_kernel, (na, nb, nodes)),
        out_shape=(
            jax.ShapeDtypeStruct((rows, m), BF16),
            jax.ShapeDtypeStruct((subs, r6, LANE), F32),
        ),
        in_specs=[hbm, hbm, vm, vm, vm, vm, pl.BlockSpec(memory_space=pltpu.SMEM)],
        out_specs=(vm, vm),
        scratch_shapes=[
            pltpu.VMEM((2, ni, ni), BF16),
            pltpu.VMEM((2, lg, total), BF16),
            pltpu.VMEM((2, ni, m), BF16),
            pltpu.VMEM((subs, 1, lg), jnp.int32),
            pltpu.VMEM((subs, lg, m), BF16),
            pltpu.VMEM((subs, lg, 2 * m), BF16),
            pltpu.VMEM((subs, lg, 2 * m), BF16),
            pltpu.VMEM((subs // 2, 2 * lg, 2 * lg), BF16),
            pltpu.VMEM((2 * lg, 2 * m), F32),
            pltpu.VMEM((rows, m), F32),
            pltpu.VMEM((rows, m), BF16),
            pltpu.VMEM((peers, ch, m), BF16),
            pltpu.VMEM((n6, LANE), F32),
            pltpu.VMEM((subs, r6, LANE), F32),
            pltpu.VMEM((nodes, r6, LANE), F32),
            dma((4,)),
            *pair(), *pair(), *pair(), *pair(),
            dma((peers,)), dma((peers,)), dma((peers,)), dma((peers,)),
            dma((subs,)), dma((subs,)), dma((peers,)), dma((peers,)),
            *pair(),
        ],
        compiler_params=pltpu.CompilerParams(
            collective_id=0, has_side_effects=True, vmem_limit_bytes=60 * 1024 * 1024
        ),
    )(
        inner_inverse[0, 0], schur_inverse[0], coupling[0], iface_index, basis_inner, basis_iface,
        node_weights,
    )
    return pl.pallas_call(
        functools.partial(factor_kernel, 1.0 / (subs * rows)),
        out_shape=(
            jax.ShapeDtypeStruct((ni, m), F32),
            jax.ShapeDtypeStruct((lg, m), F32),
        ),
        in_specs=[vm, vm],
        out_specs=(vm, vm),
        scratch_shapes=[
            pltpu.VMEM((LANE, LANE * (nbk + 1)), F32),
            pltpu.VMEM((nbk, LANE, m), F32),
            pltpu.VMEM((nbk, LANE, m), F32),
        ],
        compiler_params=pltpu.CompilerParams(vmem_limit_bytes=40 * 1024 * 1024),
    )(gram.reshape(n6, LANE), filt)


def solution(mesh):
    return jax.shard_map(
        per_device,
        mesh=mesh,
        in_specs=(
            P("node", "sub", None, None, None),
            P("node", None, "sub", None),
            P("sub", None, None),
            P("sub", None),
            P("sub", None),
            P("sub", None),
            P("node", None),
        ),
        out_specs=(P("sub", None), P("sub", None)),
        check_vma=False,
    )
```

```python
import functools
import jax
import jax.numpy as jnp
from jax import lax
from jax.experimental import pallas as pl
from jax.experimental.pallas import tpu as pltpu
from jax.sharding import PartitionSpec as P

MESH = pl.DeviceIdType.MESH
LANE = 128
F32 = jnp.float32
BF16 = jnp.bfloat16
TN = (((0,), (0,)), ((), ()))
NT = (((1,), (1,)), ((), ()))


class Gather:
    def __init__(self, na, nb, buf, send, recv):
        self.na, self.nb, self.buf, self.send, self.recv = na, nb, buf, send, recv
        node = lax.axis_index("node")
        me = lax.axis_index("sub")
        self.a = me // (2 * nb)
        self.b = (me // 2) % nb
        self.c = me % 2
        self.node = node
        self.me = me

    def slot(self, a, b, c):
        return (a * self.nb + b) * 2 + c

    def copy(self, origin, kind, place, target):
        return pltpu.make_async_remote_copy(
            src_ref=self.buf.at[origin],
            dst_ref=self.buf.at[origin],
            send_sem=self.send.at[kind, place],
            recv_sem=self.recv.at[origin],
            device_id=(self.node, target),
            device_id_type=MESH,
        )

    def routes(self, oa, ob):
        a, b = self.a, self.b
        return (
            (0, (ob == b) & (oa <= a) & (a + 1 < self.na), self.slot(a + 1, b, self.c)),
            (1, (ob == b) & (oa >= a) & (a >= 1), self.slot(a - 1, b, self.c)),
            (2, (ob <= b) & (b + 1 < self.nb), self.slot(a, b + 1, self.c)),
            (3, (ob >= b) & (b >= 1), self.slot(a, b - 1, self.c)),
        )

    def handle(self, oa, ob, own):
        origin = self.slot(oa, ob, self.c)
        place = oa * self.nb + ob
        sibling = self.slot(self.a, self.b, 1 - self.c)
        if not own:
            self.copy(origin, 4, place, sibling).wait_recv()
        for kind, cond, target in self.routes(oa, ob):

            @pl.when(cond)
            def _(kind=kind, target=target):
                self.copy(origin, kind, place, target).start()

        self.copy(origin, 4, place, sibling).start()

    def step(self, tau):
        if tau == 0:
            self.handle(self.a, self.b, True)
            return
        for tb in range(self.nb):
            t = tau - tb
            if t < 0 or t >= self.na:
                continue
            for sa in (-1, 1) if t else (1,):
                for sb in (-1, 1) if tb else (1,):
                    oa, ob = self.a + sa * t, self.b + sb * tb
                    ok = (oa >= 0) & (oa < self.na) & (ob >= 0) & (ob < self.nb)

                    @pl.when(ok)
                    def _(oa=oa, ob=ob):
                        self.handle(oa, ob, False)

    @property
    def steps(self):
        return self.na + self.nb - 1

    def finish(self):
        sibling = self.slot(self.a, self.b, 1 - self.c)

        @pl.loop(0, self.na * self.nb)
        def _(place):
            oa, ob = place // self.nb, place % self.nb
            self.copy(place * 2 + 1 - self.c, 4, place, sibling).wait_recv()
            for kind, cond, target in self.routes(oa, ob):

                @pl.when(cond)
                def _(kind=kind, target=target):
                    self.copy(place * 2 + self.c, kind, place, target).wait_send()

            self.copy(place * 2 + self.c, 4, place, sibling).wait_send()


def step_kernel(
    dims, inv_hbm, schur_hbm, couple, index, basis_in, basis_if, weights,
    filt, gbuf,
    inv, schur, solve, uv, idx_all, bas_all, con_all, sol_all, bperm, sperm, work, term, tsend, trecv, g6, grecv, nrecv,
    ld, isend, irecv, bsend, brecv, csend, crecv, ssend, srecv, tss, trs, fss, frs, gss, grs, nss, nrs, ass_, ars,
):
    na, nb, nodes = dims
    subs = na * nb * 2
    ni = inv.shape[1]
    m = basis_in.shape[1]
    lg = couple.shape[1]
    total = schur.shape[2]
    rows = ni + lg
    node = lax.axis_index("node")
    me = lax.axis_index("sub")

    load_inv = pltpu.make_async_copy(inv_hbm, inv, ld.at[0])
    load_schur = pltpu.make_async_copy(schur_hbm, schur, ld.at[1])
    put_idx = pltpu.make_async_copy(index, idx_all.at[me], ld.at[2])
    put_bas = pltpu.make_async_copy(basis_if, bas_all.at[me], ld.at[3])
    load_inv.start()
    put_idx.start()
    put_bas.start()
    load_schur.start()

    gi = Gather(na, nb, idx_all, isend, irecv)
    gb = Gather(na, nb, bas_all, bsend, brecv)
    gc = Gather(na, nb, con_all, csend, crecv)
    gs = Gather(na, nb, sol_all, ssend, srecv)

    barrier = pltpu.get_barrier_semaphore()
    a, b, c = gi.a, gi.b, gi.c
    links = (
        (a + 1 < na, gi.slot(a + 1, b, c)),
        (a >= 1, gi.slot(a - 1, b, c)),
        (b + 1 < nb, gi.slot(a, b + 1, c)),
        (b >= 1, gi.slot(a, b - 1, c)),
    )
    for cond, target in links:

        @pl.when(cond)
        def _(target=target):
            pl.semaphore_signal(barrier, inc=1, device_id=(node, target), device_id_type=MESH)

    pl.semaphore_signal(barrier, inc=1, device_id=(node, gi.slot(a, b, 1 - c)), device_id_type=MESH)
    for p in range(1, nodes):
        pl.semaphore_signal(
            barrier, inc=1, device_id=((node + p) % nodes, me), device_id_type=MESH
        )
    count = nodes
    for cond, _t in links:
        count = count + cond.astype(jnp.int32)
    pl.semaphore_wait(barrier, count)
    put_idx.wait()
    gi.step(0)
    put_bas.wait()
    gb.step(0)
    load_inv.wait()

    cr = 256
    per_part = ni // cr
    chunks = 2 * per_part
    y = basis_in[...]

    def solve_chunk(q, _):
        part = q // per_part
        r0 = pl.multiple_of((q % per_part) * cr, cr)
        out = jnp.dot(inv[part, pl.ds(r0, cr), :], y, preferred_element_type=F32)
        solve[part, pl.ds(r0, cr), :] = out.astype(BF16)
        return 0

    lax.fori_loop(0, chunks, solve_chunk, 0)
    for part in range(2):
        out = lax.dot_general(couple[...], solve[part], TN, preferred_element_type=F32)
        con_all[me, :, pl.ds(part * m, m)] = out.astype(BF16)
    gc.step(0)
    last = gi.steps - 1
    gi.step(1)
    gb.step(1)
    for tau in range(2, gi.steps):
        gi.step(tau)
        gb.step(tau)
        if tau < last:
            gc.step(tau - 1)
    gi.finish()

    load_schur.wait()
    s2 = schur[...].reshape(2 * lg, total)

    def perm_pair(q, _):
        iota = lax.broadcasted_iota(jnp.int32, (total, LANE), 0)
        hot = jnp.concatenate(
            [(iota == idx_all[2 * q + k]).astype(BF16) for k in range(2)], axis=1
        )
        got = jnp.dot(s2, hot, preferred_element_type=F32)
        sperm[q] = got.astype(BF16)
        return 0

    lax.fori_loop(0, subs // 2, perm_pair, 0)
    gc.step(last - 1)
    gb.finish()

    lanes = lax.broadcasted_iota(jnp.int32, (LANE, LANE), 1)

    def selector(row):
        rowid = jnp.broadcast_to(row, (LANE, LANE)).T
        return jnp.concatenate(
            [(lanes + LANE * k == rowid).astype(BF16) for k in range(total // LANE)], axis=1
        )

    def perm_rows(q, _):
        got = jnp.dot(
            selector(idx_all[q]), bas_all[...].reshape(total, m), preferred_element_type=F32
        )
        bperm[q] = got.astype(BF16)
        return 0

    lax.fori_loop(0, subs, perm_rows, 0)
    gc.step(last)
    gc.finish()

    work[...] = jnp.zeros_like(work)

    @pl.loop(0, subs // 2)
    def _(q):
        con = con_all[pl.ds(2 * q, 2)].reshape(2 * lg, 2 * m)
        bas = bperm[pl.ds(2 * q, 2)].reshape(2 * lg, m)
        rhs_re = (bas.astype(F32) - con[:, :m].astype(F32)).astype(BF16)
        rhs = jnp.concatenate([rhs_re, -con[:, m:]], axis=1)
        work[...] += jnp.dot(sperm[q], rhs, preferred_element_type=F32)

    sol_re = work[:lg, :m] - work[lg:, m:]
    sol_im = work[:lg, m:] + work[lg:, :m]
    sol_all[me, :, pl.ds(0, m)] = sol_re.astype(BF16)
    sol_all[me, :, pl.ds(m, m)] = sol_im.astype(BF16)
    gs.step(0)
    wr = weights[0, 0]
    wi = weights[0, 1]
    t_if = wr * sol_re.astype(BF16).astype(F32) - wi * sol_im.astype(BF16).astype(F32)
    term[pl.ds(ni, lg), :] = t_if
    tsend[pl.ds(ni, lg), :] = t_if.astype(BF16)
    sh_in, sh_if = ni // nodes, lg // nodes
    half = sh_in // 2

    def piece_of(k, i):
        if i == 2:
            return pl.ds(pl.multiple_of(ni + k * sh_if, 16), sh_if), pl.ds(sh_in, sh_if)
        return pl.ds(pl.multiple_of(k * sh_in + i * half, 16), half), pl.ds(i * half, half)

    def term_copy(p, i):
        peer = (node + p) % nodes
        src, dst = piece_of(peer, i)
        return pltpu.make_async_remote_copy(
            src_ref=tsend.at[src], dst_ref=trecv.at[p - 1, dst],
            send_sem=tss.at[p - 1, i], recv_sem=trs.at[p - 1, i],
            device_id=(peer, me), device_id_type=MESH,
        )

    def filt_copy(p, i):
        peer = (node + p) % nodes
        src, _ = piece_of(node, i)
        return pltpu.make_async_remote_copy(
            src_ref=filt.at[src], dst_ref=filt.at[src],
            send_sem=fss.at[p - 1, i], recv_sem=frs.at[p - 1, i],
            device_id=(peer, me), device_id_type=MESH,
        )

    for p in range(1, nodes):
        term_copy(p, 2).start()
    sel = selector(index[...])
    for tau in range(1, gs.steps):
        gs.step(tau)
    gs.finish()

    picked = jnp.dot(sel, sol_all[...].reshape(total, 2 * m), preferred_element_type=F32).astype(BF16)

    def uv_chunk(q, _):
        r0 = pl.multiple_of(q * cr, cr)
        cor = jnp.dot(couple[pl.ds(r0, cr), :], picked, preferred_element_type=F32)
        cor = cor.astype(BF16).astype(F32)
        uv[0, pl.ds(r0, cr), :] = (wr * cor[:, :m] - wi * cor[:, m:]).astype(BF16)
        uv[1, pl.ds(r0, cr), :] = -(wi * cor[:, :m] + wr * cor[:, m:]).astype(BF16)
        return 0

    lax.fori_loop(0, per_part, uv_chunk, 0)

    def term_piece(k, i):
        r, _ = piece_of(k, i)
        out = jnp.dot(inv[0, r, :], uv[0], preferred_element_type=F32)
        out += jnp.dot(inv[1, r, :], uv[1], preferred_element_type=F32)
        z_re = solve[0, r, :].astype(F32)
        z_im = solve[1, r, :].astype(F32)
        return wr * z_re - wi * z_im - out

    for p in range(1, nodes):
        for i in range(2):
            r, _ = piece_of((node + p) % nodes, i)
            tsend[r, :] = term_piece((node + p) % nodes, i).astype(BF16)
            term_copy(p, i).start()
    for i in range(2):
        r, _ = piece_of(node, i)
        term[r, :] = term_piece(node, i)
    own = []
    for i in (2, 0, 1):
        r, d = piece_of(node, i)
        for p in range(1, nodes):
            term_copy(p, i).wait()
        got = term[r, :]
        for p in range(1, nodes):
            got += trecv[p - 1, d, :].astype(F32)
        got = got.astype(BF16)
        filt[r, :] = got
        for p in range(1, nodes):
            filt_copy(p, i).start()
        own.append(got)
    own = jnp.concatenate([own[1], own[2], own[0]], axis=0)

    nbk = m // LANE
    at = 0
    for rb in range(nbk):
        blk = lax.dot_general(
            own[:, rb * LANE : (rb + 1) * LANE], own[:, rb * LANE :], TN, preferred_element_type=F32
        )
        for k in range(nbk - rb):
            g6[pl.ds(at * LANE, LANE), :] = blk[:, k * LANE : (k + 1) * LANE]
            at += 1
    r6 = g6.shape[0] // subs

    def piece(k):
        return pl.ds(pl.multiple_of(k * r6, 8), r6)

    def gram_copy(p):
        peer = (me + p) % subs
        return pltpu.make_async_remote_copy(
            src_ref=g6.at[piece(peer)], dst_ref=grecv.at[me],
            send_sem=gss.at[p], recv_sem=grs.at[p],
            device_id=(node, peer), device_id_type=MESH,
        )

    @pl.loop(1, subs)
    def _(p):
        gram_copy(p).start()

    grecv[me] = g6[piece(me), :]

    @pl.loop(1, subs)
    def _(p):
        gram_copy(p).wait()

    part = grecv[0]
    for k in range(1, subs):
        part += grecv[k]
    nrecv[node] = part

    def node_copy(p):
        peer = (node + p) % nodes
        return pltpu.make_async_remote_copy(
            src_ref=nrecv.at[node], dst_ref=nrecv.at[node],
            send_sem=nss.at[p - 1], recv_sem=nrs.at[p - 1],
            device_id=(peer, me), device_id_type=MESH,
        )

    for p in range(1, nodes):
        node_copy(p).start()
    for p in range(1, nodes):
        node_copy(p).wait()
    full = nrecv[0]
    for k in range(1, nodes):
        full += nrecv[k]
    gbuf[me] = full

    places = subs // 2
    spot = me // 2
    sibling = me + 1 - 2 * c

    def plane_copy(p):
        return pltpu.make_async_remote_copy(
            src_ref=gbuf.at[me], dst_ref=gbuf.at[me],
            send_sem=ass_.at[0, p], recv_sem=ars.at[me],
            device_id=(node, ((spot + p) % places) * 2 + c), device_id_type=MESH,
        )

    def from_plane(p):
        origin = ((spot + places - p) % places) * 2 + c
        return pltpu.make_async_remote_copy(
            src_ref=gbuf.at[origin], dst_ref=gbuf.at[origin],
            send_sem=ass_.at[1, p], recv_sem=ars.at[origin],
            device_id=(node, sibling), device_id_type=MESH,
        )

    def from_sibling(p):
        origin = p * 2 + 1 - c
        return pltpu.make_async_remote_copy(
            src_ref=gbuf.at[origin], dst_ref=gbuf.at[origin],
            send_sem=ass_.at[1, 0], recv_sem=ars.at[origin],
            device_id=(node, sibling), device_id_type=MESH,
        )

    @pl.loop(1, places)
    def _(p):
        plane_copy(p).start()

    from_plane(0).start()

    @pl.loop(1, places)
    def _(p):
        from_plane(p).wait_recv()
        from_plane(p).start()

    @pl.loop(0, places)
    def _(p):
        from_sibling(p).wait_recv()
        from_plane(p).wait_send()

    @pl.loop(1, places)
    def _(p):
        plane_copy(p).wait_send()

    for p in range(1, nodes):
        for i in range(3):
            filt_copy(p, i).wait()


def factor_kernel(scale, g6, filt, out_inner, out_iface, tw, urow, held, uall, wall):
    m = filt.shape[1]
    nbk = m // LANE
    width = LANE * (nbk + 1)
    row8 = lax.broadcasted_iota(jnp.int32, (8, LANE), 0)
    groups = LANE // 8
    hi = lax.Precision.HIGHEST
    at = 0
    for blk in range(nbk):
        nu = nbk - blk
        for k in range(nu):
            tw[:, k * LANE : (k + 1) * LANE] = g6[(at + k) * LANE : (at + k + 1) * LANE, :] * scale
        at += nu
        ri = lax.broadcasted_iota(jnp.int32, (LANE, LANE), 0)
        ci = lax.broadcasted_iota(jnp.int32, (LANE, LANE), 1)
        for k in range(blk + 1):
            tile = (ri == ci).astype(F32) if k == blk else jnp.zeros((LANE, LANE), F32)
            tw[:, (nu + k) * LANE : (nu + k + 1) * LANE] = tile
        for p in range(blk):
            left = uall[p, :, blk * LANE : (blk + 1) * LANE]
            tw[:, : nu * LANE] -= lax.dot_general(
                left, uall[p, :, blk * LANE :], TN, precision=hi, preferred_element_type=F32
            )
            tw[:, nu * LANE : (nu + p + 1) * LANE] -= lax.dot_general(
                left, wall[p, :, : (p + 1) * LANE], TN, precision=hi, preferred_element_type=F32
            )

        nt = nbk + 1

        def split(v):
            return [v[:, k * LANE : (k + 1) * LANE] for k in range(nt)]

        def update(tg, fac, live):
            inv, low, us = fac
            cg = [jnp.broadcast_to(tg[0][:, j : j + 1], (8, LANE)) for j in range(8)]
            for j in range(8):
                lj = cg[j] * inv[j] if live is None else cg[j] * (inv[j] * live)
                for k in range(j + 1, 8):
                    cg[k] = cg[k] - lj * low[j][k]
                tg = [t - lj * uu for t, uu in zip(tg, us[j])]
            return [pltpu.roll(tg[0], LANE - 8, 1)] + tg[1:]

        def factor(tiles):
            cols = [jnp.broadcast_to(tiles[0][:, j : j + 1], (8, LANE)) for j in range(8)]
            inv, low, us = [], [], []
            diag = jnp.ones((8, LANE), F32)
            for j in range(8):
                piv = jnp.broadcast_to(cols[j][j : j + 1, :], (8, LANE))
                r = lax.rsqrt(piv)
                r = r * (1.5 - 0.5 * piv * r * r)
                inv.append(r)
                lj = cols[j] * r
                lows = {}
                for k in range(j + 1, 8):
                    lows[k] = jnp.broadcast_to(lj[k : k + 1, :], (8, LANE))
                    cols[k] = cols[k] - lj * lows[k]
                low.append(lows)
                diag = jnp.where(row8 == j, r, diag)
                lm = jnp.where(row8 > j, lj, 0.0)
                u = [jnp.broadcast_to(t[j : j + 1, :], (8, LANE)) * r for t in tiles]
                us.append(u)
                tiles = [t - lm * uu for t, uu in zip(tiles, u)]
            return (inv, low, us), [t * diag for t in tiles]

        def keep(fac):
            inv, low, us = fac
            at = 0
            for j in range(8):
                for v in [inv[j]] + [low[j][k] for k in range(j + 1, 8)] + us[j]:
                    held[at] = v
                    at += 1

        def kept():
            at, inv, low, us = 0, [], [], []
            for j in range(8):
                inv.append(held[at])
                low.append({k: held[at + k - j] for k in range(j + 1, 8)})
                us.append([held[at + 8 - j + k] for k in range(nt)])
                at += 8 - j + nt
            return inv, low, us

        def put(r0, tiles):
            for k in range(1, nt):
                urow[pl.ds(r0, 8), k * LANE : (k + 1) * LANE] = tiles[k]

        first, rows0 = factor(split(tw[pl.ds(0, 8), :]))
        keep(first)
        put(0, rows0)

        @pl.loop(0, groups - 1)
        def _(p):
            r1 = pl.multiple_of(8 * p + 8, 8)
            fac = kept()
            ahead = update(split(tw[pl.ds(r1, 8), :]), fac, None)
            groups_now = [tw[8 * g : 8 * g + 8, :] for g in range(1, groups)]
            nxt, done = factor(ahead)
            for g in range(1, groups):
                tg = update(split(groups_now[g - 1]), fac, (g > p).astype(F32))
                for k in range(nt):
                    tw[8 * g : 8 * g + 8, k * LANE : (k + 1) * LANE] = tg[k]
            keep(nxt)
            put(r1, done)

        if nu > 1:
            uall[blk, :, (blk + 1) * LANE :] = urow[:, LANE : nu * LANE]
        wall[blk, :, : (blk + 1) * LANE] = urow[:, nu * LANE :]
        if nu > 1:
            wall[blk, :, (blk + 1) * LANE :] = jnp.zeros((LANE, (nu - 1) * LANE), F32)

    w = wall[...].reshape(m, m)
    w_hi = w.astype(BF16)
    w_lo = (w - w_hi.astype(F32)).astype(BF16)

    def apply(rows):
        out = lax.dot_general(rows, w_hi, NT, preferred_element_type=F32)
        return out + lax.dot_general(rows, w_lo, NT, preferred_element_type=F32)

    ni = out_inner.shape[0]

    @pl.loop(0, ni // LANE)
    def _(q):
        r0 = pl.multiple_of(q * LANE, LANE)
        out_inner[pl.ds(r0, LANE), :] = apply(filt[pl.ds(r0, LANE), :])

    out_iface[...] = apply(filt[pl.ds(ni, LANE), :])


def per_device(
    inner_inverse, schur_inverse, coupling, iface_index, basis_inner, basis_iface, node_weights
):
    subs, nodes = lax.axis_size("sub"), lax.axis_size("node")
    na = 4
    nb = subs // (2 * na)
    ni, m = basis_inner.shape
    lg = basis_iface.shape[0]
    total = schur_inverse.shape[3]
    rows = ni + lg
    ch = rows // nodes
    nbk = m // LANE
    n6 = nbk * (nbk + 1) // 2 * LANE
    r6 = n6 // subs
    vm = pl.BlockSpec(memory_space=pltpu.VMEM)
    hbm = pl.BlockSpec(memory_space=pl.ANY)
    dma = pltpu.SemaphoreType.DMA

    def pair():
        return [dma((5, subs // 2)), dma((subs,))]

    peers = max(nodes - 1, 1)
    filt, gram = pl.pallas_call(
        functools.partial(step_kernel, (na, nb, nodes)),
        out_shape=(
            jax.ShapeDtypeStruct((rows, m), BF16),
            jax.ShapeDtypeStruct((subs, r6, LANE), F32),
        ),
        in_specs=[hbm, hbm, vm, vm, vm, vm, pl.BlockSpec(memory_space=pltpu.SMEM)],
        out_specs=(vm, vm),
        scratch_shapes=[
            pltpu.VMEM((2, ni, ni), BF16),
            pltpu.VMEM((2, lg, total), BF16),
            pltpu.VMEM((2, ni, m), BF16),
            pltpu.VMEM((2, ni, m), BF16),
            pltpu.VMEM((subs, 1, lg), jnp.int32),
            pltpu.VMEM((subs, lg, m), BF16),
            pltpu.VMEM((subs, lg, 2 * m), BF16),
            pltpu.VMEM((subs, lg, 2 * m), BF16),
            pltpu.VMEM((subs, lg, m), BF16),
            pltpu.VMEM((subs // 2, 2 * lg, 2 * lg), BF16),
            pltpu.VMEM((2 * lg, 2 * m), F32),
            pltpu.VMEM((rows, m), F32),
            pltpu.VMEM((rows, m), BF16),
            pltpu.VMEM((peers, ch, m), BF16),
            pltpu.VMEM((n6, LANE), F32),
            pltpu.VMEM((subs, r6, LANE), F32),
            pltpu.VMEM((nodes, r6, LANE), F32),
            dma((4,)),
            *pair(), *pair(), *pair(), *pair(),
            dma((peers, 3)), dma((peers, 3)), dma((peers, 3)), dma((peers, 3)),
            dma((subs,)), dma((subs,)), dma((peers,)), dma((peers,)),
            *pair(),
        ],
        compiler_params=pltpu.CompilerParams(
            collective_id=0, has_side_effects=True, vmem_limit_bytes=60 * 1024 * 1024
        ),
    )(
        inner_inverse[0, 0], schur_inverse[0], coupling[0], iface_index, basis_inner, basis_iface,
        node_weights,
    )
    return pl.pallas_call(
        functools.partial(factor_kernel, 1.0 / (subs * rows)),
        out_shape=(
            jax.ShapeDtypeStruct((ni, m), F32),
            jax.ShapeDtypeStruct((lg, m), F32),
        ),
        in_specs=[vm, vm],
        out_specs=(vm, vm),
        scratch_shapes=[
            pltpu.VMEM((LANE, LANE * (nbk + 1)), F32),
            pltpu.VMEM((LANE, LANE * (nbk + 1)), F32),
            pltpu.VMEM((36 + 8 * (nbk + 1), 8, LANE), F32),
            pltpu.VMEM((nbk, LANE, m), F32),
            pltpu.VMEM((nbk, LANE, m), F32),
        ],
        compiler_params=pltpu.CompilerParams(vmem_limit_bytes=40 * 1024 * 1024),
    )(gram.reshape(n6, LANE), filt)


def solution(mesh):
    return jax.shard_map(
        per_device,
        mesh=mesh,
        in_specs=(
            P("node", "sub", None, None, None),
            P("node", None, "sub", None),
            P("sub", None, None),
            P("sub", None),
            P("sub", None),
            P("sub", None),
            P("node", None),
        ),
        out_specs=(P("sub", None), P("sub", None)),
        check_vma=False,
    )
```
